32 devices in a mesh: mem: 8 (over z, x), feat: 4 (over y, core).
Axes of the slice: x: 2, y: 2, z: 4, core: 2. Of those that a mesh axis runs over, the one named last changes fastest.
Arguments:
- events: bfloat16 [2048, 32, 256], P('mem'), may hold values from -6 to 6
- w_in: bfloat16 [256, 1024], P(None, 'feat'), may hold values from -0.375 to 0.375
- w_out: bfloat16 [1024, 256], P('feat'), may hold values from -0.1875 to 0.1875
- probe_vectors: bfloat16 [2048, 256], P(('mem', 'feat')), may hold values from -8 to 8
- key_queue: bfloat16 [65536, 256], P('mem'), may hold values from -1 to 1
- target_position: int32 [2048], P(('mem', 'feat')), may hold values from 0 to 65535
- pointer: int32 [1], replicated, may hold values from 0 to 65535
Outputs:
- loss: float32 [2048], P(('mem', 'feat'))
- probe_derivative: float32 [2048, 256], P(('mem', 'feat'))
- new_memory: bfloat16 [65536, 256], P('mem')
The draws below stay inside these ranges and needn't reach their ends.
All inputs are finite; a program needn't handle non-finite values.
Results may differ from the reference program's by a relative error of at most 0.0017.
Values may be sent and summed in bfloat16 or wider, within the bound.
A program may use at most 64 MiB of HBM per device.

```python
import jax
import jax.numpy as jnp
from jax import lax

D = 256
HID = 1024
EVENTS = 32
SESS_DEV = 256
SLOT_DEV = 8192
QUERIES = 2048
SESSIONS = 2048
SLOTS = 65536
N_MEM = 8


def shared_directions(key):
    norm_factor = 1.0 / jnp.sqrt(jnp.float32(D))
    first = jax.random.truncated_normal(jax.random.fold_in(key, 7), -6.0, 6.0, (16, D), jnp.float32) * norm_factor
    second = jax.random.truncated_normal(jax.random.fold_in(key, 8), -6.0, 6.0, (16, D), jnp.float32) * norm_factor
    first = jnp.clip(first, -0.9, 0.9)
    second = jnp.clip(second, -0.9, 0.9)
    return (first, 0.99 * first + 0.1 * second)


def draw_key_queue(key, part):
    values_drawn = jax.random.truncated_normal(jax.random.fold_in(key, 1), -6.0, 6.0, (SLOTS, D), jnp.float32) / 16.0
    first, twins = shared_directions(key)
    planted_rows = jnp.arange(16, dtype=jnp.int32) * (SLOTS // 16) + 3
    values_drawn = values_drawn.at[planted_rows].set(first)
    values_drawn = values_drawn.at[planted_rows + SLOTS // 32 + 5].set(twins)
    return jnp.clip(values_drawn, -1.0, 1.0).astype(jnp.bfloat16)


def draw_probe_vectors(key, part):
    values_drawn = jax.random.truncated_normal(jax.random.fold_in(key, 2), -6.0, 6.0, (QUERIES, D), jnp.float32) * 0.25
    first, twins = shared_directions(key)
    planted_rows = jnp.arange(16, dtype=jnp.int32) * (QUERIES // 16)
    strength = 9.0 + 9.0 * jnp.arange(16, dtype=jnp.float32) / 15.0
    values_drawn = values_drawn.at[planted_rows].set(jnp.clip(strength[:, None] * first, -8.0, 8.0))
    return values_drawn.astype(jnp.bfloat16)


def touch_ends(drawn, stream_key, low, high):
    extent = drawn.shape
    index_at = [jax.random.randint(jax.random.fold_in(stream_key, axis), (), 0, extent[axis]) for axis in range(len(extent))]
    drawn = drawn.at[tuple(index_at)].set(low)
    longest = extent.index(max(extent))
    index_at[longest] = (index_at[longest] + 1) % extent[longest]
    return drawn.at[tuple(index_at)].set(high)


def levels(own_key, dims, split, low, top_value):
    gain, own = 1.0, jax.random.fold_in(own_key, 6)
    for axis_at, shards_of in split:
        steps = jnp.exp(jax.random.uniform(jax.random.fold_in(own, axis_at), (shards_of,), jnp.float32, low / len(split), top_value / len(split)))
        gain = gain * jnp.repeat(steps, dims[axis_at] // shards_of).reshape([-1 if axis == axis_at else 1 for axis in range(len(dims))])
    return gain


def gaussian(rng, dims, spread, limit, cuts=(), kind=jnp.bfloat16):
    drawn = jax.random.normal(rng, dims, jnp.float32) * spread
    if len(cuts) > 0:
        drawn = levels(rng, dims, cuts, -0.22, 0.18) * drawn
    return jnp.clip(drawn, min=-limit, max=limit).astype(kind)


def setup_inputs(seed: int = 0) -> dict:
    arg_keys = jax.random.split(jax.random.key(seed), 8)
    return {
        "events": gaussian(arg_keys[0], (SESSIONS, EVENTS, D), 1.0, 6.0, ((0, 8),)),
        "w_in": gaussian(arg_keys[1], (D, HID), D ** -0.5, 0.375, ((1, 4),)),
        "w_out": gaussian(arg_keys[2], (HID, D), HID ** -0.5, 0.1875, ((0, 4),)),
        "probe_vectors": draw_probe_vectors(jax.random.fold_in(arg_keys[7], 71), 0),
        "key_queue": draw_key_queue(jax.random.fold_in(arg_keys[7], 71), 0),
        "target_position": touch_ends(jax.random.randint(arg_keys[5], (QUERIES,), 0, SLOTS), jax.random.fold_in(arg_keys[5], 1), 0, SLOTS - 1).astype(jnp.int32),
        "pointer": jax.random.randint(arg_keys[6], (1,), 0, SLOTS).astype(jnp.int32),
    }


inverse_softness = 14.0
epsilon = 1e-06

def encode_block(session_block, w_in, w_out):
    flattened = session_block.reshape(session_block.shape[0] * EVENTS, D)
    activation = jax.nn.gelu(jnp.dot(flattened, w_in, preferred_element_type=jnp.float32))
    pooled = lax.optimization_barrier(jnp.mean(activation.reshape(session_block.shape[0], EVENTS, HID), axis=1)).astype(jnp.bfloat16)
    raw_key = jnp.dot(pooled, w_out, preferred_element_type=jnp.float32)
    scaled = raw_key * lax.rsqrt(lax.optimization_barrier(jnp.mean(raw_key * raw_key, axis=1, keepdims=True)) + epsilon) / 16.0
    return scaled.astype(jnp.bfloat16)

def reference(events, w_in, w_out, probe_vectors, key_queue, target_position, pointer):

    def encode_one(session_block):
        return encode_block(session_block, w_in, w_out)
    keys = lax.map(encode_one, events.reshape(N_MEM, SESS_DEV, EVENTS, D)).reshape(N_MEM * SESS_DEV, D)
    query_count = probe_vectors.shape[0]
    slot_blocks = key_queue.reshape(N_MEM, SLOT_DEV, D)
    block_starts = jnp.arange(N_MEM, dtype=jnp.int32) * SLOT_DEV
    positions = jnp.arange(SLOT_DEV, dtype=jnp.int32)

    def first_pass(carry, item):
        running_max, running_sum, positive_score = carry
        queue_position_span, first_slot = item
        similarity_table = jnp.dot(probe_vectors, queue_position_span.T, preferred_element_type=jnp.float32) * inverse_softness
        new_max = jnp.maximum(running_max, lax.optimization_barrier(jnp.max(similarity_table, axis=1)))
        running_sum = running_sum * jnp.exp(running_max - new_max) + lax.optimization_barrier(jnp.sum(jnp.exp(similarity_table - new_max[:, None]), axis=1))
        hit = positions[None, :] == (target_position - first_slot)[:, None]
        positive_score = positive_score + lax.optimization_barrier(jnp.sum(jnp.where(hit, similarity_table, 0.0), axis=1))
        return ((new_max, running_sum, positive_score), None)
    start_carry = (jnp.full((query_count,), -jnp.inf, jnp.float32), jnp.zeros((query_count,), jnp.float32), jnp.zeros((query_count,), jnp.float32))
    (top, total, positive_score), unused = lax.scan(first_pass, start_carry, (slot_blocks, block_starts))
    loss = top + jnp.log(total) - positive_score

    def second_pass(collected_denominator, queue_position_span):
        similarity_table = jnp.dot(probe_vectors, queue_position_span.T, preferred_element_type=jnp.float32) * inverse_softness
        weights = (jnp.exp(similarity_table - top[:, None]) / total[:, None]).astype(jnp.bfloat16)
        return (collected_denominator + jnp.dot(weights, queue_position_span, preferred_element_type=jnp.float32), None)
    collected_denominator, unused = lax.scan(second_pass, jnp.zeros((query_count, D), jnp.float32), slot_blocks)
    probe_derivative = inverse_softness * (collected_denominator - jnp.take(key_queue, target_position, axis=0).astype(jnp.float32))
    slot_count = N_MEM * SLOT_DEV
    slot_ids = jnp.arange(slot_count, dtype=jnp.int32)
    offsets = (slot_ids - pointer[0]) % slot_count
    picked = jnp.take(keys, jnp.minimum(offsets, keys.shape[0] - 1), axis=0)
    new_memory = jnp.where((offsets < keys.shape[0])[:, None], picked, key_queue)
    return (loss, probe_derivative, new_memory)
```

```python
import functools

import jax
import jax.numpy as jnp
from jax import lax
from jax.experimental import pallas as pl
from jax.experimental.pallas import tpu as pltpu
from jax.sharding import PartitionSpec as P

inverse_softness = 14.0
epsilon = 1e-06
log2e = 1.4426950408889634
MESH = pl.DeviceIdType.MESH
ANY = pl.BlockSpec(memory_space=pl.ANY)
VMEM = pl.BlockSpec(memory_space=pltpu.VMEM)


def step_kernel(
    n, nf, per, ev_chunk, slot_block, q_chunk,
    ev_hbm, w_in_ref, w_out_ref, probe_ref, queue_hbm, target_ref,
    loss_ref, grad_ref, keys_ref,
    ev, queue, q_all, t_all, pooled, partial, part_in, pos, m_s, l_s, acc, paired,
    stat, stat_in, gout, g_in,
    ev_sem, queue_sem, q_ss, q_rs, t_ss, t_rs, p_ss, p_rs, k_ss, k_rs, y_ss, y_rs, c_ss, c_rs,
    s_ss, s_rs, g_ss, g_rs,
):
    me = lax.axis_index("mem")
    mf = lax.axis_index("feat")
    own = probe_ref.shape[0]
    rows_q = q_all.shape[0]
    slots, width = queue.shape
    ev_rows = ev.shape[0]
    n_ev, n_blk = ev_rows // ev_chunk, slots // slot_block
    sessions = pooled.shape[0]
    part_rows = sessions // nf

    def ev_copy(i):
        span = pl.ds(pl.multiple_of(i * ev_chunk, ev_chunk), ev_chunk)
        return pltpu.make_async_copy(ev_hbm.at[span], ev.at[span], ev_sem.at[i])

    def queue_copy(i):
        span = pl.ds(pl.multiple_of(i * slot_block, slot_block), slot_block)
        return pltpu.make_async_copy(queue_hbm.at[span], queue.at[span], queue_sem.at[i])

    for i in range(n_ev):
        ev_copy(i).start()
    for i in range(n_blk):
        queue_copy(i).start()

    def mem_peer(k):
        return (lax.rem(me + k, n), mf)

    def mem_from(k):
        return lax.rem(me + n - k, n)

    def feat_peer(k):
        return (me, lax.rem(mf + k, nf))

    barrier = pltpu.get_barrier_semaphore()
    for k in range(1, n):
        pl.semaphore_signal(barrier, inc=1, device_id=mem_peer(k), device_id_type=MESH)
    for k in range(1, nf):
        pl.semaphore_signal(barrier, inc=1, device_id=feat_peer(k), device_id_type=MESH)
    pl.semaphore_wait(barrier, n - 1 + nf - 1)

    def remote(src, dst, ss, rs, to):
        return pltpu.make_async_remote_copy(
            src_ref=src, dst_ref=dst, send_sem=ss, recv_sem=rs, device_id=to, device_id_type=MESH
        )

    own_span = pl.ds(pl.multiple_of(me * own, own), own)
    q_copies, t_copies = [], []
    for k in range(1, n):
        q_copies.append(remote(probe_ref, q_all.at[own_span], q_ss.at[k], q_rs.at[k], mem_peer(k)))
        t_copies.append(remote(target_ref, t_all.at[me], t_ss.at[k], t_rs.at[k], mem_peer(k)))
    for a in q_copies + t_copies:
        a.start()
    q_all[own_span, :] = probe_ref[...]
    t_all[me] = target_ref[...]

    events_of = ev_chunk // (sessions // n_ev)
    c1 = 0.7978845608028654
    c2 = c1 * 0.044715

    def encode(i, carry):
        ev_copy(i).wait()
        rows = ev[pl.ds(pl.multiple_of(i * ev_chunk, ev_chunk), ev_chunk), :]
        x = jnp.dot(rows, w_in_ref[...], preferred_element_type=jnp.float32)
        t = jnp.tanh(x * (c1 + c2 * (x * x)))
        y = x * t + x
        y = y.reshape(ev_chunk // events_of, events_of, y.shape[1])
        mean = jnp.sum(y, axis=1) * (0.5 / events_of)
        s = ev_chunk // events_of
        pooled[pl.ds(pl.multiple_of(i * s, s), s), :] = mean.astype(jnp.bfloat16)
        return carry

    lax.fori_loop(0, n_ev, encode, 0)
    partial[...] = jnp.dot(pooled[...], w_out_ref[...], preferred_element_type=jnp.float32)

    def part_span(f):
        return pl.ds(pl.multiple_of(f * part_rows, part_rows), part_rows)

    p_copies = []
    for k in range(1, nf):
        to = feat_peer(k)
        p_copies.append(
            remote(partial.at[part_span(to[1])], part_in.at[k], p_ss.at[k], p_rs.at[k], to)
        )
        p_copies[-1].start()

    for a in q_copies + t_copies:
        a.wait()

    diag = lax.broadcasted_iota(jnp.int32, (own, own), 0) == lax.broadcasted_iota(
        jnp.int32, (own, own), 1
    )
    for j in range(n):
        row = t_all[j].astype(jnp.float32)
        col = jnp.sum(jnp.where(diag, jnp.broadcast_to(row, (own, own)), 0.0), axis=1, keepdims=True)
        local = col.astype(jnp.int32) - me * slots
        pos[j * own : (j + 1) * own, :] = jnp.broadcast_to(local, (own, 128))

    m_s[...] = jnp.full(m_s.shape, -jnp.inf, jnp.float32)
    l_s[...] = jnp.zeros(l_s.shape, jnp.float32)
    acc[...] = jnp.zeros(acc.shape, jnp.float32)
    paired[...] = jnp.zeros(paired.shape, jnp.float32)
    scale2 = inverse_softness * log2e

    def attend(b, carry):
        queue_copy(b).wait()
        kb = queue[pl.ds(pl.multiple_of(b * slot_block, slot_block), slot_block), :]
        for c in range(rows_q // q_chunk):
            rs = slice(c * q_chunk, (c + 1) * q_chunk)
            s = lax.dot_general(
                q_all[rs, :], kb, (((1,), (1,)), ((), ())), preferred_element_type=jnp.float32
            )
            m_old = m_s[rs, :1]
            m_new = jnp.maximum(m_old, jnp.max(s, axis=1, keepdims=True))
            p = jnp.exp2((s - m_new) * scale2)
            alpha = jnp.exp2((m_old - m_new) * scale2)
            m_s[rs, :] = jnp.broadcast_to(m_new, (q_chunk, 128))
            l_new = l_s[rs, :1] * alpha + jnp.sum(p, axis=1, keepdims=True)
            l_s[rs, :] = jnp.broadcast_to(l_new, (q_chunk, 128))
            acc[rs, :] = acc[rs, :] * alpha + jnp.dot(
                p.astype(jnp.bfloat16), kb, preferred_element_type=jnp.float32
            )
            hit = lax.broadcasted_iota(jnp.int32, s.shape, 1) == (pos[rs, :1] - b * slot_block)
            paired[rs, :] += jnp.dot(
                jnp.where(hit, 1.0, 0.0).astype(jnp.bfloat16), kb, preferred_element_type=jnp.float32
            )
        return carry

    half = n_blk // 2
    lax.fori_loop(0, half, attend, 0)

    for a in p_copies:
        a.wait()
    raw = partial[part_span(mf), :]
    for k in range(1, nf):
        raw = raw + part_in[k]
    scaled = raw * lax.rsqrt(jnp.mean(raw * raw, axis=1, keepdims=True) + epsilon) / 16.0

    def key_span(m, f):
        return pl.ds(pl.multiple_of((m * nf + f) * part_rows, part_rows), part_rows)

    mine = key_span(me, mf)
    keys_ref[mine, :] = scaled.astype(jnp.bfloat16)

    def to_same(span, ss, rs, to):
        return remote(keys_ref.at[span], keys_ref.at[span], ss, rs, to)

    k_copies = [to_same(mine, k_ss.at[k], k_rs.at[k], mem_peer(k)) for k in range(1, n)]
    for a in k_copies:
        a.start()
    far_feat = lax.rem(mf + nf // 2, nf)
    far = (me, far_feat)
    near = (me, mf + 1 - 2 * lax.rem(mf, 2))
    y_copies = [to_same(mine, y_ss.at[0], y_rs.at[0], far)]
    c_copies = [to_same(mine, c_ss.at[0], c_rs.at[0], near)]
    y_copies[0].start()
    c_copies[0].start()

    lax.fori_loop(half, n_blk, attend, 0)

    lane = lax.broadcasted_iota(jnp.int32, m_s.shape, 1)
    pos_score = jnp.sum(q_all[...].astype(jnp.float32) * paired[...], axis=1, keepdims=True)
    packed = jnp.where(lane == 0, m_s[...], jnp.where(lane == 1, l_s[...], pos_score))
    stat[...] = packed.T[:8, :]
    s_copies = [
        remote(stat, stat_in.at[k], s_ss.at[k], s_rs.at[k], mem_peer(k)) for k in range(1, n)
    ]
    for a in s_copies:
        a.start()

    for k in range(1, n):
        k_copies[k - 1].wait_recv()
        span = key_span(mem_from(k), mf)
        y_copies.append(to_same(span, y_ss.at[k], y_rs.at[k], far))
        c_copies.append(to_same(span, c_ss.at[k], c_rs.at[k], near))
        y_copies[-1].start()
        c_copies[-1].start()

    for a in s_copies:
        a.wait()
    mine_stat = stat[...]
    top = mine_stat[0:1, :]
    for k in range(1, n):
        top = jnp.maximum(top, stat_in[k][0:1, :])
    total = mine_stat[1:2, :] * jnp.exp2((mine_stat[0:1, :] - top) * scale2)
    score = mine_stat[2:3, :]
    for k in range(1, n):
        other = stat_in[k]
        total = total + other[1:2, :] * jnp.exp2((other[0:1, :] - top) * scale2)
        score = score + other[2:3, :]
    loss_row = (top - score) * inverse_softness + jnp.log(total)
    loss = loss_row[:, :own]
    for j in range(1, n):
        loss = jnp.where(me == j, loss_row[:, j * own : (j + 1) * own], loss)
    loss_ref[...] = loss
    factor = jnp.exp2((mine_stat[0:1, :] - top) * scale2) / total
    factor = jnp.broadcast_to(factor, (128, rows_q)).T[:, :1]
    gout[...] = inverse_softness * (acc[...] * factor - paired[...])
    g_copies = []
    for k in range(1, n):
        to = mem_peer(k)
        span = pl.ds(pl.multiple_of(to[0] * own, own), own)
        g_copies.append(remote(gout.at[span], g_in.at[k], g_ss.at[k], g_rs.at[k], to))
        g_copies[-1].start()

    for k in range(n):
        y_copies[k].wait_recv()
        span = key_span(mem_from(k), far_feat)
        c_copies.append(to_same(span, c_ss.at[n + k], c_rs.at[n + k], near))
        c_copies[-1].start()

    grad = gout[own_span, :]
    for k in range(1, n):
        g_copies[k - 1].wait()
        grad = grad + g_in[k]
    grad_ref[...] = grad
    for a in k_copies + y_copies:
        a.wait_send()
    for a in c_copies:
        a.wait()


def fill_kernel(block, pad, start_ref, keys_ref, queue_ref, out_ref, rolled):
    start = start_ref[0]
    count = keys_ref.shape[0]
    first = pl.program_id(0) * block
    phase = jnp.bitwise_and(start, 15)
    local = pl.num_programs(0) * block

    @pl.when((pl.program_id(0) == 0) & (start < local) & (start + count > 0))
    def _():
        tile = 256

        for c in range(count // tile + 1):
            lo = max(c * tile - 16, 0)
            hi = min(c * tile + tile, count)
            x = keys_ref[lo:hi, :].astype(jnp.float32)
            if c == 0:
                x = jnp.concatenate([jnp.zeros((16, x.shape[1]), jnp.float32), x], axis=0)
            if c == count // tile:
                x = jnp.concatenate([x, jnp.zeros((16, x.shape[1]), jnp.float32)], axis=0)
            x = pltpu.roll(x, phase, 0)[16:, :]
            rolled[pad + c * tile : pad + c * tile + x.shape[0], :] = x.astype(jnp.bfloat16)

    inside = (first < start + count) & (first + block > start)

    @pl.when(inside)
    def _():
        at = pl.multiple_of(pad + first - (start - phase), 16)
        row = lax.broadcasted_iota(jnp.int32, (block, queue_ref.shape[1]), 0) + (first - start)
        take = (row >= 0) & (row < count)
        new = rolled[pl.ds(at, block), :].astype(jnp.float32)
        old = queue_ref[...].astype(jnp.float32)
        out_ref[...] = jnp.where(take, new, old).astype(jnp.bfloat16)

    @pl.when(jnp.logical_not(inside))
    def _():
        out_ref[...] = queue_ref[...]


def shards(events, w_in, w_out, probe_vectors, key_queue, target_position, pointer):
    n, nf = lax.axis_size("mem"), lax.axis_size("feat")
    sessions, per, depth = events.shape
    own, width = probe_vectors.shape
    slots = key_queue.shape[0]
    rows_q = own * n
    hidden = w_in.shape[1]
    flat = events.reshape(sessions * per, depth)
    ev_chunk = min(1024, flat.shape[0])
    slot_block = min(1024, slots)
    q_chunk = min(256, rows_q)
    part_rows = sessions // nf
    f32, bf16 = jnp.float32, jnp.bfloat16
    dma = pltpu.SemaphoreType.DMA
    loss, grad, keys = pl.pallas_call(
        functools.partial(step_kernel, n, nf, per, ev_chunk, slot_block, q_chunk),
        out_shape=(
            jax.ShapeDtypeStruct((1, own), f32),
            jax.ShapeDtypeStruct((own, width), f32),
            jax.ShapeDtypeStruct((sessions * n, width), bf16),
        ),
        in_specs=[ANY, VMEM, VMEM, VMEM, ANY, VMEM],
        out_specs=(VMEM, VMEM, VMEM),
        scratch_shapes=[
            pltpu.VMEM(flat.shape, bf16),
            pltpu.VMEM(key_queue.shape, bf16),
            pltpu.VMEM((rows_q, width), bf16),
            pltpu.VMEM((n, 1, own), jnp.int32),
            pltpu.VMEM((sessions, hidden), bf16),
            pltpu.VMEM((sessions, width), f32),
            pltpu.VMEM((nf, part_rows, width), f32),
            pltpu.VMEM((rows_q, 128), jnp.int32),
            pltpu.VMEM((rows_q, 128), f32),
            pltpu.VMEM((rows_q, 128), f32),
            pltpu.VMEM((rows_q, width), f32),
            pltpu.VMEM((rows_q, width), f32),
            pltpu.VMEM((8, rows_q), f32),
            pltpu.VMEM((n, 8, rows_q), f32),
            pltpu.VMEM((rows_q, width), f32),
            pltpu.VMEM((n, own, width), f32),
            dma((flat.shape[0] // ev_chunk,)),
            dma((slots // slot_block,)),
            dma((n,)), dma((n,)), dma((n,)), dma((n,)),
            dma((nf,)), dma((nf,)),
            dma((n,)), dma((n,)),
            dma((n,)), dma((n,)),
            dma((2 * n,)), dma((2 * n,)),
            dma((n,)), dma((n,)),
            dma((n,)), dma((n,)),
        ],
        compiler_params=pltpu.CompilerParams(
            collective_id=0, has_side_effects=True, vmem_limit_bytes=56 * 1024 * 1024
        ),
        name="step",
    )(flat, w_in, w_out, probe_vectors, key_queue, target_position.reshape(1, own))

    slots_total = slots * n
    start = lax.rem(pointer - lax.axis_index("mem") * slots + slots_total, slots_total)
    count = sessions * n
    start = jnp.where(start > slots_total - count, start - slots_total, start)
    block = min(1024, slots)
    new_memory = pl.pallas_call(
        functools.partial(fill_kernel, block, block),
        grid=(slots // block,),
        out_shape=jax.ShapeDtypeStruct(key_queue.shape, bf16),
        in_specs=[
            pl.BlockSpec(memory_space=pltpu.SMEM),
            VMEM,
            pl.BlockSpec((block, width), lambda i: (i, 0)),
        ],
        out_specs=pl.BlockSpec((block, width), lambda i: (i, 0)),
        scratch_shapes=[pltpu.VMEM((count + 2 * block + 16, width), bf16)],
        compiler_params=pltpu.CompilerParams(vmem_limit_bytes=32 * 1024 * 1024),
        name="fill",
    )(start, keys, key_queue)
    return (loss.reshape(own), grad, new_memory)


def solution(mesh):
    placed = (
        P("mem", None, None),
        P(None, "feat"),
        P("feat", None),
        P(("mem", "feat"), None),
        P("mem", None),
        P(("mem", "feat")),
        P(),
    )
    return jax.shard_map(
        shards,
        mesh=mesh,
        in_specs=placed,
        out_specs=(P(("mem", "feat")), P(("mem", "feat"), None), P("mem", None)),
        check_vma=False,
    )
```

```python
import functools

import jax
import jax.numpy as jnp
from jax import lax
from jax.experimental import pallas as pl
from jax.experimental.pallas import tpu as pltpu
from jax.sharding import PartitionSpec as P

inverse_softness = 14.0
epsilon = 1e-06
log2e = 1.4426950408889634
MESH = pl.DeviceIdType.MESH
ANY = pl.BlockSpec(memory_space=pl.ANY)
VMEM = pl.BlockSpec(memory_space=pltpu.VMEM)
HBM = pl.BlockSpec(memory_space=pltpu.HBM)


def step_kernel(
    n, nf, ev_chunk, slot_block, q_chunk,
    ev_hbm, w_in_ref, w_out_ref, probe_ref, queue_hbm, target_ref,
    loss_ref, grad_ref, keys_ref,
    ev, queue, q_all, t_all, pooled, partial, part_in, pos, m_s, l_s, acc,
    pair_out, pair_in, stat_out, stat_in, gout, g_in,
    ev_sem, queue_sem, q_ss, q_rs, t_ss, t_rs, p_ss, p_rs, k_ss, k_rs, y_ss, y_rs, c_ss, c_rs,
    s_ss, s_rs, g_ss, g_rs, h_ss, h_rs,
):
    me = lax.axis_index("mem")
    mf = lax.axis_index("feat")
    own = probe_ref.shape[0]
    rows_q = q_all.shape[0]
    slots, width = queue.shape
    ev_rows = ev.shape[0]
    n_ev, n_blk = ev_rows // ev_chunk, slots // slot_block
    sessions = pooled.shape[0]
    part_rows = sessions // nf

    def ev_copy(i):
        span = pl.ds(pl.multiple_of(i * ev_chunk, ev_chunk), ev_chunk)
        return pltpu.make_async_copy(ev_hbm.at[span], ev.at[span], ev_sem.at[i])

    def queue_copy(i):
        span = pl.ds(pl.multiple_of(i * slot_block, slot_block), slot_block)
        return pltpu.make_async_copy(queue_hbm.at[span], queue.at[span], queue_sem.at[i])

    partner = me + 1 - 2 * lax.rem(me, 2)

    def mem_peer(k):
        return (lax.rem(me + k, n), mf)

    def feat_peer(k):
        return (me, lax.rem(mf + k, nf))

    def block_id(i):
        return lax.rem(me + n - i, n) if i % 2 == 0 else lax.rem(partner + n - (i - 1), n)

    barrier = pltpu.get_barrier_semaphore()
    for k in range(1, n):
        pl.semaphore_signal(barrier, inc=1, device_id=mem_peer(k), device_id_type=MESH)
    for k in range(1, nf):
        pl.semaphore_signal(barrier, inc=1, device_id=feat_peer(k), device_id_type=MESH)
    for i in range(n_ev):
        ev_copy(i).start()
    for i in range(n_blk):
        queue_copy(i).start()

    def own_span(m):
        return pl.ds(pl.multiple_of(m * own, own), own)

    q_all[own_span(me), :] = probe_ref[...]
    t_all[me] = target_ref[...]
    pl.semaphore_wait(barrier, n - 1 + nf - 1)

    def remote(src, dst, ss, rs, to):
        return pltpu.make_async_remote_copy(
            src_ref=src, dst_ref=dst, send_sem=ss, recv_sem=rs, device_id=to, device_id_type=MESH
        )

    t_copies = [
        remote(target_ref, t_all.at[me], t_ss.at[k], t_rs.at[k], mem_peer(k)) for k in range(1, n)
    ]
    q_copies = {
        k: remote(probe_ref, q_all.at[own_span(me)], q_ss.at[k], q_rs.at[k], mem_peer(k))
        for k in range(2, n, 2)
    }
    q_copies[1] = remote(
        probe_ref, q_all.at[own_span(me)], q_ss.at[1], q_rs.at[1], (partner, mf)
    )
    for a in q_copies.values():
        a.start()
    for a in t_copies:
        a.start()

    events_of = ev_rows // sessions
    c1 = 0.7978845608028654
    c2 = c1 * 0.044715

    def encode(i, carry):
        ev_copy(i).wait()
        rows = ev[pl.ds(pl.multiple_of(i * ev_chunk, ev_chunk), ev_chunk), :]
        x = jnp.dot(rows, w_in_ref[...], preferred_element_type=jnp.float32)
        t = jnp.tanh(x * (c1 + c2 * (x * x)))
        y = x * t + x
        y = y.reshape(ev_chunk // events_of, events_of, y.shape[1])
        mean = jnp.sum(y, axis=1) * (0.5 / events_of)
        s = ev_chunk // events_of
        pooled[pl.ds(pl.multiple_of(i * s, s), s), :] = mean.astype(jnp.bfloat16)
        return carry

    lax.fori_loop(0, n_ev, encode, 0)
    partial[...] = jnp.dot(pooled[...], w_out_ref[...], preferred_element_type=jnp.float32)

    def part_span(f):
        return pl.ds(pl.multiple_of(f * part_rows, part_rows), part_rows)

    p_copies = []
    for k in range(1, nf):
        to = feat_peer(k)
        p_copies.append(
            remote(partial.at[part_span(to[1])], part_in.at[k], p_ss.at[k], p_rs.at[k], to)
        )
        p_copies[-1].start()

    for k in range(2, n, 2):
        q_copies[k].wait_recv()
        span = own_span(block_id(k))
        q_copies[k + 1] = remote(
            q_all.at[span], q_all.at[span], q_ss.at[k + 1], q_rs.at[k + 1], (partner, mf)
        )
        q_copies[k + 1].start()
    for a in t_copies:
        a.wait()

    diag = lax.broadcasted_iota(jnp.int32, (own, own), 0) == lax.broadcasted_iota(
        jnp.int32, (own, own), 1
    )

    def as_column(row):
        wide = jnp.broadcast_to(row, (own, own))
        return jnp.sum(jnp.where(diag, wide, 0.0), axis=1, keepdims=True)

    for j in range(n):
        local = as_column(t_all[j].astype(jnp.float32)).astype(jnp.int32) - me * slots
        pos[j * own : (j + 1) * own, :] = jnp.broadcast_to(local, (own, 128))

    acc[...] = jnp.zeros(acc.shape, jnp.float32)

    def pick(b, carry):
        queue_copy(b).wait()
        kb = queue[pl.ds(pl.multiple_of(b * slot_block, slot_block), slot_block), :]
        for c in range(rows_q // q_chunk):
            rs = slice(c * q_chunk, (c + 1) * q_chunk)
            at = lax.broadcasted_iota(jnp.int32, (q_chunk, slot_block), 1)
            hit = at == (pos[rs, :1] - b * slot_block)
            acc[rs, :] += jnp.dot(
                jnp.where(hit, 1.0, 0.0).astype(jnp.bfloat16), kb, preferred_element_type=jnp.float32
            )
        return carry

    lax.fori_loop(0, n_blk, pick, 0)
    pair_out[...] = acc[...].astype(jnp.bfloat16)
    h_copies = []
    for k in range(1, n):
        to = mem_peer(k)
        h_copies.append(
            remote(pair_out.at[own_span(to[0])], pair_in.at[k], h_ss.at[k], h_rs.at[k], to)
        )
        h_copies[-1].start()

    for k in range(1, n, 2):
        q_copies[k].wait_recv()

    m_s[...] = jnp.full(m_s.shape, -jnp.inf, jnp.float32)
    l_s[...] = jnp.zeros(l_s.shape, jnp.float32)
    acc[...] = jnp.zeros(acc.shape, jnp.float32)
    scale2 = inverse_softness * log2e

    def attend(b, carry):
        kb = queue[pl.ds(pl.multiple_of(b * slot_block, slot_block), slot_block), :]
        for c in range(rows_q // q_chunk):
            rs = slice(c * q_chunk, (c + 1) * q_chunk)
            s = lax.dot_general(
                q_all[rs, :], kb, (((1,), (1,)), ((), ())), preferred_element_type=jnp.float32
            )
            m_old = m_s[rs, :1]
            m_new = jnp.maximum(m_old, jnp.max(s, axis=1, keepdims=True))
            p = jnp.exp2((s - m_new) * scale2)
            alpha = jnp.exp2((m_old - m_new) * scale2)
            m_s[rs, :] = jnp.broadcast_to(m_new, (q_chunk, 128))
            l_new = l_s[rs, :1] * alpha + jnp.sum(p, axis=1, keepdims=True)
            l_s[rs, :] = jnp.broadcast_to(l_new, (q_chunk, 128))
            acc[rs, :] = acc[rs, :] * alpha + jnp.dot(
                p.astype(jnp.bfloat16), kb, preferred_element_type=jnp.float32
            )
        return carry

    stage_a, stage_b = n_blk // 8, (5 * n_blk) // 8
    lax.fori_loop(0, stage_a, attend, 0)

    for a in p_copies:
        a.wait()
    raw = partial[part_span(mf), :]
    for k in range(1, nf):
        raw = raw + part_in[k]
    scaled = raw * lax.rsqrt(jnp.mean(raw * raw, axis=1, keepdims=True) + epsilon) / 16.0

    def key_span(m, f):
        return pl.ds(pl.multiple_of((m * nf + f) * part_rows, part_rows), part_rows)

    mine = key_span(me, mf)
    keys_ref[mine, :] = scaled.astype(jnp.bfloat16)
    far_feat = lax.rem(mf + nf // 2, nf)
    far = (me, far_feat)
    near = (me, mf + 1 - 2 * lax.rem(mf, 2))

    def to_same(span, ss, rs, i, to):
        a = remote(keys_ref.at[span], keys_ref.at[span], ss.at[i], rs.at[i], to)
        a.start()
        return a

    k_copies = {k: to_same(mine, k_ss, k_rs, k, mem_peer(k)) for k in range(2, n, 2)}
    k_copies[1] = to_same(mine, k_ss, k_rs, 1, (partner, mf))
    y_copies = {0: to_same(mine, y_ss, y_rs, 0, far)}
    c_copies = {0: to_same(mine, c_ss, c_rs, 0, near)}

    lax.fori_loop(stage_a, stage_b, attend, 0)

    for k in range(2, n, 2):
        k_copies[k].wait_recv()
        span = key_span(block_id(k), mf)
        k_copies[k + 1] = to_same(span, k_ss, k_rs, k + 1, (partner, mf))
        y_copies[k] = to_same(span, y_ss, y_rs, k, far)
        c_copies[k] = to_same(span, c_ss, c_rs, k, near)

    lax.fori_loop(stage_b, n_blk, attend, 0)

    gout[...] = acc[...].astype(jnp.bfloat16)
    g_copies = []
    for k in range(1, n):
        to = mem_peer(k)
        g_copies.append(remote(gout.at[own_span(to[0])], g_in.at[k], g_ss.at[k], g_rs.at[k], to))
        g_copies[-1].start()
    lane = lax.broadcasted_iota(jnp.int32, m_s.shape, 1)
    packed = jnp.where(lane == 0, m_s[...], l_s[...]).T
    for j in range(n):
        stat_out[j, 0:2, :] = packed[0:2, j * own : (j + 1) * own]
    s_copies = []
    for k in range(1, n):
        to = mem_peer(k)
        s_copies.append(remote(stat_out.at[to[0]], stat_in.at[k], s_ss.at[k], s_rs.at[k], to))
        s_copies[-1].start()

    for i in range(1, n, 2):
        k_copies[i].wait_recv()
        span = key_span(block_id(i), mf)
        y_copies[i] = to_same(span, y_ss, y_rs, i, far)
        c_copies[i] = to_same(span, c_ss, c_rs, i, near)

    paired = pair_out[own_span(me), :].astype(jnp.float32)
    for a in h_copies:
        a.wait()
    for k in range(1, n):
        paired = paired + pair_in[k].astype(jnp.float32)
    score = jnp.sum(probe_ref[...].astype(jnp.float32) * paired, axis=1, keepdims=True)
    score = jnp.sum(
        jnp.where(diag, jnp.broadcast_to(score, (own, own)), 0.0), axis=0, keepdims=True
    )

    order = [0] + list(range(2, n, 2)) + list(range(1, n, 2))
    for i in order:
        y_copies[i].wait_recv()
        c_copies[n + i] = to_same(key_span(block_id(i), far_feat), c_ss, c_rs, n + i, near)

    for a in s_copies:
        a.wait()
    stats = [stat_out[me]] + [stat_in[k] for k in range(1, n)]
    top = stats[0][0:1, :]
    for st in stats[1:]:
        top = jnp.maximum(top, st[0:1, :])
    powers = [jnp.exp2((st[0:1, :] - top) * scale2) for st in stats]
    total = stats[0][1:2, :] * powers[0]
    for st, w in zip(stats[1:], powers[1:]):
        total = total + st[1:2, :] * w
    loss_ref[...] = (top - score) * inverse_softness + jnp.log(total)
    grad = acc[own_span(me), :] * as_column(powers[0] / total)
    for k in range(1, n):
        g_copies[k - 1].wait()
        grad = grad + g_in[k].astype(jnp.float32) * as_column(powers[k] / total)
    grad_ref[...] = inverse_softness * (grad - paired)

    for a in list(q_copies.values()) + list(k_copies.values()) + list(y_copies.values()):
        a.wait_send()
    for a in c_copies.values():
        a.wait()


def fill_kernel(
    block, start_ref, keys_hbm, queue_ref, loss_in, grad_in,
    loss_ref, grad_ref, out_hbm,
    keys, rolled, merged, keys_sem, out_sem,
):
    start = start_ref[0]
    count = keys.shape[0]
    slots, width = queue_ref.shape
    phase = jnp.bitwise_and(start, 15)
    blocks = slots // block
    here = (start < slots) & (start + count > 0)
    keys_copy = pltpu.make_async_copy(keys_hbm, keys, keys_sem)

    @pl.when(here)
    def _():
        keys_copy.start()

    def spans(i):
        return slice(i * block, (i + 1) * block)

    def inside(i):
        return (i * block < start + count) & ((i + 1) * block > start)

    def plain(i):
        return pltpu.make_async_copy(queue_ref.at[spans(i)], out_hbm.at[spans(i)], out_sem.at[i])

    for i in range(blocks):

        @pl.when(jnp.logical_not(inside(i)))
        def _():
            plain(i).start()

    loss_ref[...] = loss_in[...]
    grad_ref[...] = grad_in[...]

    @pl.when(here)
    def _():
        keys_copy.wait()
        tile = min(256, count)
        for c in range(count // tile + 1):
            lo = max(c * tile - 16, 0)
            hi = min(c * tile + tile, count)
            x = keys[lo:hi, :].astype(jnp.float32)
            if c == 0:
                x = jnp.concatenate([jnp.zeros((16, width), jnp.float32), x], axis=0)
            if c == count // tile:
                x = jnp.concatenate([x, jnp.zeros((16, width), jnp.float32)], axis=0)
            x = pltpu.roll(x, phase, 0)[16:, :]
            at = block + c * tile
            rolled[at : at + x.shape[0], :] = x.astype(jnp.bfloat16)

    for i in range(blocks):

        @pl.when(inside(i))
        def _():
            at = pl.multiple_of(block + i * block - (start - phase), 16)
            row = lax.broadcasted_iota(jnp.int32, (block, width), 0) + (i * block - start)
            take = (row >= 0) & (row < count)
            new = rolled[pl.ds(at, block), :].astype(jnp.float32)
            old = queue_ref[spans(i), :].astype(jnp.float32)
            merged[spans(i), :] = jnp.where(take, new, old).astype(jnp.bfloat16)
            pltpu.make_async_copy(
                merged.at[spans(i)], out_hbm.at[spans(i)], out_sem.at[i]
            ).start()

    for i in range(blocks):
        plain(i).wait()


def shards(events, w_in, w_out, probe_vectors, key_queue, target_position, pointer):
    n, nf = lax.axis_size("mem"), lax.axis_size("feat")
    sessions, per, depth = events.shape
    own, width = probe_vectors.shape
    slots = key_queue.shape[0]
    rows_q = own * n
    hidden = w_in.shape[1]
    flat = events.reshape(sessions * per, depth)
    ev_chunk = min(1024, flat.shape[0])
    slot_block = min(1024, slots)
    q_chunk = min(256, rows_q)
    part_rows = sessions // nf
    f32, bf16 = jnp.float32, jnp.bfloat16
    dma = pltpu.SemaphoreType.DMA
    loss, grad, keys = pl.pallas_call(
        functools.partial(step_kernel, n, nf, ev_chunk, slot_block, q_chunk),
        out_shape=(
            jax.ShapeDtypeStruct((1, own), f32),
            jax.ShapeDtypeStruct((own, width), f32),
            jax.ShapeDtypeStruct((sessions * n, width), bf16),
        ),
        in_specs=[ANY, VMEM, VMEM, VMEM, ANY, VMEM],
        out_specs=(VMEM, VMEM, VMEM),
        scratch_shapes=[
            pltpu.VMEM(flat.shape, bf16),
            pltpu.VMEM(key_queue.shape, bf16),
            pltpu.VMEM((rows_q, width), bf16),
            pltpu.VMEM((n, 1, own), jnp.int32),
            pltpu.VMEM((sessions, hidden), bf16),
            pltpu.VMEM((sessions, width), f32),
            pltpu.VMEM((nf, part_rows, width), f32),
            pltpu.VMEM((rows_q, 128), jnp.int32),
            pltpu.VMEM((rows_q, 128), f32),
            pltpu.VMEM((rows_q, 128), f32),
            pltpu.VMEM((rows_q, width), f32),
            pltpu.VMEM((rows_q, width), bf16),
            pltpu.VMEM((n, own, width), bf16),
            pltpu.VMEM((n, 4, own), f32),
            pltpu.VMEM((n, 4, own), f32),
            pltpu.VMEM((rows_q, width), bf16),
            pltpu.VMEM((n, own, width), bf16),
            dma((flat.shape[0] // ev_chunk,)),
            dma((slots // slot_block,)),
            dma((n,)), dma((n,)), dma((n,)), dma((n,)),
            dma((nf,)), dma((nf,)),
            dma((n,)), dma((n,)),
            dma((n,)), dma((n,)),
            dma((2 * n,)), dma((2 * n,)),
            dma((n,)), dma((n,)),
            dma((n,)), dma((n,)),
            dma((n,)), dma((n,)),
        ],
        compiler_params=pltpu.CompilerParams(
            collective_id=0, has_side_effects=True, vmem_limit_bytes=56 * 1024 * 1024
        ),
        name="step",
    )(flat, w_in, w_out, probe_vectors, key_queue, target_position.reshape(1, own))

    slots_total = slots * n
    start = lax.rem(pointer - lax.axis_index("mem") * slots + slots_total, slots_total)
    count = sessions * n
    start = jnp.where(start > slots_total - count, start - slots_total, start)
    block = min(512, slots)
    loss, grad, new_memory = pl.pallas_call(
        functools.partial(fill_kernel, block),
        out_shape=(
            jax.ShapeDtypeStruct((1, own), f32),
            jax.ShapeDtypeStruct((own, width), f32),
            jax.ShapeDtypeStruct(key_queue.shape, bf16),
        ),
        in_specs=[pl.BlockSpec(memory_space=pltpu.SMEM), HBM, VMEM, VMEM, VMEM],
        out_specs=(VMEM, VMEM, HBM),
        scratch_shapes=[
            pltpu.VMEM((count, width), bf16),
            pltpu.VMEM((count + 2 * block + 16, width), bf16),
            pltpu.VMEM(key_queue.shape, bf16),
            dma,
            dma((slots // block,)),
        ],
        compiler_params=pltpu.CompilerParams(vmem_limit_bytes=61000 * 1024),
        name="fill",
    )(start, keys, key_queue, loss, grad)
    return (loss.reshape(own), grad, new_memory)


def solution(mesh):
    placed = (
        P("mem", None, None),
        P(None, "feat"),
        P("feat", None),
        P(("mem", "feat"), None),
        P("mem", None),
        P(("mem", "feat")),
        P(),
    )
    return jax.shard_map(
        shards,
        mesh=mesh,
        in_specs=placed,
        out_specs=(P(("mem", "feat")), P(("mem", "feat"), None), P("mem", None)),
        check_vma=False,
    )
```

```python
import functools

import jax
import jax.numpy as jnp
from jax import lax
from jax.experimental import pallas as pl
from jax.experimental.pallas import tpu as pltpu
from jax.sharding import PartitionSpec as P

inverse_softness = 14.0
epsilon = 1e-06
log2e = 1.4426950408889634
MESH = pl.DeviceIdType.MESH
ANY = pl.BlockSpec(memory_space=pl.ANY)
VMEM = pl.BlockSpec(memory_space=pltpu.VMEM)
HBM = pl.BlockSpec(memory_space=pltpu.HBM)


def step_kernel(
    n, nf, ev_chunk, slot_block, q_chunk,
    ev_hbm, w_in_hbm, w_out_hbm, probe_hbm, queue_hbm, target_ref,
    loss_ref, grad_ref, keys_ref,
    w_in_ref, w_out_ref, probe_ref, load_sem, ev, queue, q_all, t_all, pooled, partial, part_in, pos, m_s, l_s, acc,
    pair_out, pair_in, stat_out, stat_in, gout, g_in,
    ev_sem, queue_sem, q_ss, q_rs, t_ss, t_rs, p_ss, p_rs, k_ss, k_rs, y_ss, y_rs, c_ss, c_rs,
    s_ss, s_rs, g_ss, g_rs, h_ss, h_rs,
):
    me = lax.axis_index("mem")
    mf = lax.axis_index("feat")
    own = probe_ref.shape[0]
    loads = [
        pltpu.make_async_copy(a, b, load_sem.at[i])
        for i, (a, b) in enumerate(
            ((probe_hbm, probe_ref), (w_in_hbm, w_in_ref), (w_out_hbm, w_out_ref))
        )
    ]
    rows_q = q_all.shape[0]
    slots, width = queue.shape
    ev_rows = ev.shape[0]
    n_ev, n_blk = ev_rows // ev_chunk, slots // slot_block
    sessions = pooled.shape[0]
    part_rows = sessions // nf

    def ev_copy(i):
        span = pl.ds(pl.multiple_of(i * ev_chunk, ev_chunk), ev_chunk)
        return pltpu.make_async_copy(ev_hbm.at[span], ev.at[span], ev_sem.at[i])

    def queue_copy(i):
        span = pl.ds(pl.multiple_of(i * slot_block, slot_block), slot_block)
        return pltpu.make_async_copy(queue_hbm.at[span], queue.at[span], queue_sem.at[i])

    partner = me + 1 - 2 * lax.rem(me, 2)

    def mem_peer(k):
        return (lax.rem(me + k, n), mf)

    def feat_peer(k):
        return (me, lax.rem(mf + k, nf))

    def block_id(i):
        return lax.rem(me + n - i, n) if i % 2 == 0 else lax.rem(partner + n - (i - 1), n)

    barrier = pltpu.get_barrier_semaphore()
    for k in range(1, n):
        pl.semaphore_signal(barrier, inc=1, device_id=mem_peer(k), device_id_type=MESH)
    for k in range(1, nf):
        pl.semaphore_signal(barrier, inc=1, device_id=feat_peer(k), device_id_type=MESH)
    for a in loads:
        a.start()
    for i in range(n_ev):
        ev_copy(i).start()
    for i in range(n_blk):
        queue_copy(i).start()
    loads[0].wait()

    def own_span(m):
        return pl.ds(pl.multiple_of(m * own, own), own)

    q_all[own_span(me), :] = probe_ref[...]
    t_all[me] = target_ref[...]
    pl.semaphore_wait(barrier, n - 1 + nf - 1)

    def remote(src, dst, ss, rs, to):
        return pltpu.make_async_remote_copy(
            src_ref=src, dst_ref=dst, send_sem=ss, recv_sem=rs, device_id=to, device_id_type=MESH
        )

    t_copies = [
        remote(target_ref, t_all.at[me], t_ss.at[k], t_rs.at[k], mem_peer(k)) for k in range(1, n)
    ]
    q_copies = {
        k: remote(probe_ref, q_all.at[own_span(me)], q_ss.at[k], q_rs.at[k], mem_peer(k))
        for k in range(2, n, 2)
    }
    q_copies[1] = remote(
        probe_ref, q_all.at[own_span(me)], q_ss.at[1], q_rs.at[1], (partner, mf)
    )
    for a in q_copies.values():
        a.start()
    for a in t_copies:
        a.start()

    events_of = ev_rows // sessions
    c1 = 0.7978845608028654
    c2 = c1 * 0.044715

    def encode(i, carry):
        ev_copy(i).wait()
        rows = ev[pl.ds(pl.multiple_of(i * ev_chunk, ev_chunk), ev_chunk), :]
        x = jnp.dot(rows, w_in_ref[...], preferred_element_type=jnp.float32)
        t = jnp.tanh(x * (c1 + c2 * (x * x)))
        y = x * t + x
        y = y.reshape(ev_chunk // events_of, events_of, y.shape[1])
        mean = jnp.sum(y, axis=1) * (0.5 / events_of)
        s = ev_chunk // events_of
        pooled[pl.ds(pl.multiple_of(i * s, s), s), :] = mean.astype(jnp.bfloat16)
        return carry

    loads[1].wait()
    loads[2].wait()
    lax.fori_loop(0, n_ev, encode, 0)
    partial[...] = jnp.dot(pooled[...], w_out_ref[...], preferred_element_type=jnp.float32)

    def part_span(f):
        return pl.ds(pl.multiple_of(f * part_rows, part_rows), part_rows)

    p_copies = []
    for k in range(1, nf):
        to = feat_peer(k)
        p_copies.append(
            remote(partial.at[part_span(to[1])], part_in.at[k], p_ss.at[k], p_rs.at[k], to)
        )
        p_copies[-1].start()

    for k in range(2, n, 2):
        q_copies[k].wait_recv()
        span = own_span(block_id(k))
        q_copies[k + 1] = remote(
            q_all.at[span], q_all.at[span], q_ss.at[k + 1], q_rs.at[k + 1], (partner, mf)
        )
        q_copies[k + 1].start()
    for a in t_copies:
        a.wait()

    diag = lax.broadcasted_iota(jnp.int32, (own, own), 0) == lax.broadcasted_iota(
        jnp.int32, (own, own), 1
    )

    def as_column(row):
        wide = jnp.broadcast_to(row, (own, own))
        return jnp.sum(jnp.where(diag, wide, 0.0), axis=1, keepdims=True)

    for j in range(n):
        local = as_column(t_all[j].astype(jnp.float32)).astype(jnp.int32) - me * slots
        pos[j * own : (j + 1) * own, :] = jnp.broadcast_to(local, (own, 128))

    acc[...] = jnp.zeros(acc.shape, jnp.float32)

    def pick(b, carry):
        queue_copy(b).wait()
        kb = queue[pl.ds(pl.multiple_of(b * slot_block, slot_block), slot_block), :]
        for c in range(rows_q // q_chunk):
            rs = slice(c * q_chunk, (c + 1) * q_chunk)
            at = lax.broadcasted_iota(jnp.int32, (q_chunk, slot_block), 1)
            hit = at == (pos[rs, :1] - b * slot_block)
            acc[rs, :] += jnp.dot(
                jnp.where(hit, 1.0, 0.0).astype(jnp.bfloat16), kb, preferred_element_type=jnp.float32
            )
        return carry

    lax.fori_loop(0, n_blk, pick, 0)
    pair_out[...] = acc[...].astype(jnp.bfloat16)
    h_copies = []
    for k in range(1, n):
        to = mem_peer(k)
        h_copies.append(
            remote(pair_out.at[own_span(to[0])], pair_in.at[k], h_ss.at[k], h_rs.at[k], to)
        )
        h_copies[-1].start()

    for k in range(1, n, 2):
        q_copies[k].wait_recv()

    m_s[...] = jnp.full(m_s.shape, -jnp.inf, jnp.float32)
    l_s[...] = jnp.zeros(l_s.shape, jnp.float32)
    acc[...] = jnp.zeros(acc.shape, jnp.float32)
    scale2 = inverse_softness * log2e

    def attend(b, carry):
        kb = queue[pl.ds(pl.multiple_of(b * slot_block, slot_block), slot_block), :]
        for c in range(rows_q // q_chunk):
            rs = slice(c * q_chunk, (c + 1) * q_chunk)
            s = lax.dot_general(
                q_all[rs, :], kb, (((1,), (1,)), ((), ())), preferred_element_type=jnp.float32
            )
            m_old = m_s[rs, :1]
            m_new = jnp.maximum(m_old, jnp.max(s, axis=1, keepdims=True))
            p = jnp.exp2((s - m_new) * scale2)
            alpha = jnp.exp2((m_old - m_new) * scale2)
            m_s[rs, :] = jnp.broadcast_to(m_new, (q_chunk, 128))
            l_new = l_s[rs, :1] * alpha + jnp.sum(p, axis=1, keepdims=True)
            l_s[rs, :] = jnp.broadcast_to(l_new, (q_chunk, 128))
            acc[rs, :] = acc[rs, :] * alpha + jnp.dot(
                p.astype(jnp.bfloat16), kb, preferred_element_type=jnp.float32
            )
        return carry

    stage_a, stage_b = n_blk // 8, (5 * n_blk) // 8
    lax.fori_loop(0, stage_a, attend, 0)

    for a in p_copies:
        a.wait()
    raw = partial[part_span(mf), :]
    for k in range(1, nf):
        raw = raw + part_in[k]
    scaled = raw * lax.rsqrt(jnp.mean(raw * raw, axis=1, keepdims=True) + epsilon) / 16.0

    def key_span(m, f):
        return pl.ds(pl.multiple_of((m * nf + f) * part_rows, part_rows), part_rows)

    mine = key_span(me, mf)
    keys_ref[mine, :] = scaled.astype(jnp.bfloat16)
    far_feat = lax.rem(mf + nf // 2, nf)
    far = (me, far_feat)
    near = (me, mf + 1 - 2 * lax.rem(mf, 2))

    def to_same(span, ss, rs, i, to):
        a = remote(keys_ref.at[span], keys_ref.at[span], ss.at[i], rs.at[i], to)
        a.start()
        return a

    k_copies = {k: to_same(mine, k_ss, k_rs, k, mem_peer(k)) for k in range(2, n, 2)}
    k_copies[1] = to_same(mine, k_ss, k_rs, 1, (partner, mf))
    y_copies = {0: to_same(mine, y_ss, y_rs, 0, far)}
    c_copies = {0: to_same(mine, c_ss, c_rs, 0, near)}

    lax.fori_loop(stage_a, stage_b, attend, 0)

    for k in range(2, n, 2):
        k_copies[k].wait_recv()
        span = key_span(block_id(k), mf)
        k_copies[k + 1] = to_same(span, k_ss, k_rs, k + 1, (partner, mf))
        y_copies[k] = to_same(span, y_ss, y_rs, k, far)
        c_copies[k] = to_same(span, c_ss, c_rs, k, near)

    lax.fori_loop(stage_b, n_blk, attend, 0)

    gout[...] = acc[...].astype(jnp.bfloat16)
    g_copies = []
    for k in range(1, n):
        to = mem_peer(k)
        g_copies.append(remote(gout.at[own_span(to[0])], g_in.at[k], g_ss.at[k], g_rs.at[k], to))
        g_copies[-1].start()
    lane = lax.broadcasted_iota(jnp.int32, m_s.shape, 1)
    packed = jnp.where(lane == 0, m_s[...], l_s[...]).T
    for j in range(n):
        stat_out[j, 0:2, :] = packed[0:2, j * own : (j + 1) * own]
    s_copies = []
    for k in range(1, n):
        to = mem_peer(k)
        s_copies.append(remote(stat_out.at[to[0]], stat_in.at[k], s_ss.at[k], s_rs.at[k], to))
        s_copies[-1].start()

    for i in range(1, n, 2):
        k_copies[i].wait_recv()
        span = key_span(block_id(i), mf)
        y_copies[i] = to_same(span, y_ss, y_rs, i, far)
        c_copies[i] = to_same(span, c_ss, c_rs, i, near)

    paired = pair_out[own_span(me), :].astype(jnp.float32)
    for a in h_copies:
        a.wait()
    for k in range(1, n):
        paired = paired + pair_in[k].astype(jnp.float32)
    score = jnp.sum(probe_ref[...].astype(jnp.float32) * paired, axis=1, keepdims=True)
    score = jnp.sum(
        jnp.where(diag, jnp.broadcast_to(score, (own, own)), 0.0), axis=0, keepdims=True
    )

    order = [0] + list(range(2, n, 2)) + list(range(1, n, 2))
    for i in order:
        y_copies[i].wait_recv()
        c_copies[n + i] = to_same(key_span(block_id(i), far_feat), c_ss, c_rs, n + i, near)

    for a in s_copies:
        a.wait()
    stats = [stat_out[me]] + [stat_in[k] for k in range(1, n)]
    top = stats[0][0:1, :]
    for st in stats[1:]:
        top = jnp.maximum(top, st[0:1, :])
    powers = [jnp.exp2((st[0:1, :] - top) * scale2) for st in stats]
    total = stats[0][1:2, :] * powers[0]
    for st, w in zip(stats[1:], powers[1:]):
        total = total + st[1:2, :] * w
    loss_ref[...] = (top - score) * inverse_softness + jnp.log(total)
    grad = acc[own_span(me), :] * as_column(powers[0] / total)
    for k in range(1, n):
        g_copies[k - 1].wait()
        grad = grad + g_in[k].astype(jnp.float32) * as_column(powers[k] / total)
    grad_ref[...] = inverse_softness * (grad - paired)

    for a in list(q_copies.values()) + list(k_copies.values()) + list(y_copies.values()):
        a.wait_send()
    for a in c_copies.values():
        a.wait()


def fill_kernel(
    block, start_ref, keys_hbm, queue_hbm, loss_in, grad_in,
    loss_ref, grad_ref, out_hbm,
    keys, rolled, held, keys_sem, in_sem, out_sem,
):
    start = start_ref[0]
    count = keys.shape[0]
    slots, width = held.shape
    phase = jnp.bitwise_and(start, 15)
    blocks = slots // block
    here = (start < slots) & (start + count > 0)
    keys_copy = pltpu.make_async_copy(keys_hbm, keys, keys_sem)

    @pl.when(here)
    def _():
        keys_copy.start()

    def spans(i):
        return slice(i * block, (i + 1) * block)

    def inside(i):
        return (i * block < start + count) & ((i + 1) * block > start)

    def load(i):
        return pltpu.make_async_copy(queue_hbm.at[spans(i)], held.at[spans(i)], in_sem.at[i])

    def put(i):
        return pltpu.make_async_copy(held.at[spans(i)], out_hbm.at[spans(i)], out_sem.at[i])

    for i in range(blocks):
        load(i).start()
    for i in range(blocks):
        load(i).wait()

        @pl.when(jnp.logical_not(inside(i)))
        def _():
            put(i).start()

    loss_ref[...] = loss_in[...]
    grad_ref[...] = grad_in[...]

    @pl.when(here)
    def _():
        keys_copy.wait()
        tile = min(256, count)
        for c in range(count // tile + 1):
            lo = max(c * tile - 16, 0)
            hi = min(c * tile + tile, count)
            x = keys[lo:hi, :].astype(jnp.float32)
            if c == 0:
                x = jnp.concatenate([jnp.zeros((16, width), jnp.float32), x], axis=0)
            if c == count // tile:
                x = jnp.concatenate([x, jnp.zeros((16, width), jnp.float32)], axis=0)
            x = pltpu.roll(x, phase, 0)[16:, :]
            at = block + c * tile
            rolled[at : at + x.shape[0], :] = x.astype(jnp.bfloat16)

    for i in range(blocks):

        @pl.when(inside(i))
        def _():
            at = pl.multiple_of(block + i * block - (start - phase), 16)
            row = lax.broadcasted_iota(jnp.int32, (block, width), 0) + (i * block - start)
            take = (row >= 0) & (row < count)
            new = rolled[pl.ds(at, block), :].astype(jnp.float32)
            old = held[spans(i), :].astype(jnp.float32)
            held[spans(i), :] = jnp.where(take, new, old).astype(jnp.bfloat16)
            put(i).start()

    for i in range(blocks):
        put(i).wait()


def shards(events, w_in, w_out, probe_vectors, key_queue, target_position, pointer):
    n, nf = lax.axis_size("mem"), lax.axis_size("feat")
    sessions, per, depth = events.shape
    own, width = probe_vectors.shape
    slots = key_queue.shape[0]
    rows_q = own * n
    hidden = w_in.shape[1]
    flat = events.reshape(sessions * per, depth)
    ev_chunk = min(1024, flat.shape[0])
    slot_block = min(1024, slots)
    q_chunk = min(256, rows_q)
    part_rows = sessions // nf
    f32, bf16 = jnp.float32, jnp.bfloat16
    dma = pltpu.SemaphoreType.DMA
    loss, grad, keys = pl.pallas_call(
        functools.partial(step_kernel, n, nf, ev_chunk, slot_block, q_chunk),
        out_shape=(
            jax.ShapeDtypeStruct((1, own), f32),
            jax.ShapeDtypeStruct((own, width), f32),
            jax.ShapeDtypeStruct((sessions * n, width), bf16),
        ),
        in_specs=[ANY, ANY, ANY, ANY, ANY, VMEM],
        out_specs=(VMEM, VMEM, VMEM),
        scratch_shapes=[
            pltpu.VMEM(w_in.shape, bf16),
            pltpu.VMEM(w_out.shape, bf16),
            pltpu.VMEM(probe_vectors.shape, bf16),
            dma((3,)),
            pltpu.VMEM(flat.shape, bf16),
            pltpu.VMEM(key_queue.shape, bf16),
            pltpu.VMEM((rows_q, width), bf16),
            pltpu.VMEM((n, 1, own), jnp.int32),
            pltpu.VMEM((sessions, hidden), bf16),
            pltpu.VMEM((sessions, width), f32),
            pltpu.VMEM((nf, part_rows, width), f32),
            pltpu.VMEM((rows_q, 128), jnp.int32),
            pltpu.VMEM((rows_q, 128), f32),
            pltpu.VMEM((rows_q, 128), f32),
            pltpu.VMEM((rows_q, width), f32),
            pltpu.VMEM((rows_q, width), bf16),
            pltpu.VMEM((n, own, width), bf16),
            pltpu.VMEM((n, 4, own), f32),
            pltpu.VMEM((n, 4, own), f32),
            pltpu.VMEM((rows_q, width), bf16),
            pltpu.VMEM((n, own, width), bf16),
            dma((flat.shape[0] // ev_chunk,)),
            dma((slots // slot_block,)),
            dma((n,)), dma((n,)), dma((n,)), dma((n,)),
            dma((nf,)), dma((nf,)),
            dma((n,)), dma((n,)),
            dma((n,)), dma((n,)),
            dma((2 * n,)), dma((2 * n,)),
            dma((n,)), dma((n,)),
            dma((n,)), dma((n,)),
            dma((n,)), dma((n,)),
        ],
        compiler_params=pltpu.CompilerParams(
            collective_id=0, has_side_effects=True, vmem_limit_bytes=56 * 1024 * 1024
        ),
        name="step",
    )(flat, w_in, w_out, probe_vectors, key_queue, target_position.reshape(1, own))

    slots_total = slots * n
    start = lax.rem(pointer - lax.axis_index("mem") * slots + slots_total, slots_total)
    count = sessions * n
    start = jnp.where(start > slots_total - count, start - slots_total, start)
    block = min(512, slots)
    loss, grad, new_memory = pl.pallas_call(
        functools.partial(fill_kernel, block),
        out_shape=(
            jax.ShapeDtypeStruct((1, own), f32),
            jax.ShapeDtypeStruct((own, width), f32),
            jax.ShapeDtypeStruct(key_queue.shape, bf16),
        ),
        in_specs=[pl.BlockSpec(memory_space=pltpu.SMEM), HBM, HBM, VMEM, VMEM],
        out_specs=(VMEM, VMEM, HBM),
        scratch_shapes=[
            pltpu.VMEM((count, width), bf16),
            pltpu.VMEM((count + 2 * block + 16, width), bf16),
            pltpu.VMEM(key_queue.shape, bf16),
            dma,
            dma((slots // block,)),
            dma((slots // block,)),
        ],
        compiler_params=pltpu.CompilerParams(vmem_limit_bytes=61000 * 1024),
        name="fill",
    )(start, keys, key_queue, loss, grad)
    return (loss.reshape(own), grad, new_memory)


def solution(mesh):
    placed = (
        P("mem", None, None),
        P(None, "feat"),
        P("feat", None),
        P(("mem", "feat"), None),
        P("mem", None),
        P(("mem", "feat")),
        P(),
    )
    return jax.shard_map(
        shards,
        mesh=mesh,
        in_specs=placed,
        out_specs=(P(("mem", "feat")), P(("mem", "feat"), None), P("mem", None)),
        check_vma=False,
    )
```

```python
import functools

import jax
import jax.numpy as jnp
from jax import lax
from jax.experimental import pallas as pl
from jax.experimental.pallas import tpu as pltpu
from jax.sharding import PartitionSpec as P

inverse_softness = 14.0
epsilon = 1e-06
log2e = 1.4426950408889634
MESH = pl.DeviceIdType.MESH
ANY = pl.BlockSpec(memory_space=pl.ANY)
VMEM = pl.BlockSpec(memory_space=pltpu.VMEM)
HBM = pl.BlockSpec(memory_space=pltpu.HBM)


def step_kernel(
    n, nf, ev_chunk, slot_block, q_chunk,
    ev_hbm, w_in_ref, w_out_ref, probe_ref, queue_hbm, target_ref,
    loss_ref, grad_ref, keys_ref,
    ev, queue, q_all, t_all, pooled, partial, part_in, pos, m_s, l_s, acc,
    pair_out, pair_in, stat_out, stat_in, gout, g_in,
    ev_sem, queue_sem, q_ss, q_rs, t_ss, t_rs, p_ss, p_rs, k_ss, k_rs, y_ss, y_rs, c_ss, c_rs,
    s_ss, s_rs, g_ss, g_rs, h_ss, h_rs,
):
    me = lax.axis_index("mem")
    mf = lax.axis_index("feat")
    own = probe_ref.shape[0]
    rows_q = q_all.shape[0]
    slots, width = queue.shape
    ev_rows = ev.shape[0]
    n_ev, n_blk = ev_rows // ev_chunk, slots // slot_block
    sessions = pooled.shape[0]
    part_rows = sessions // nf

    def ev_copy(i):
        span = pl.ds(pl.multiple_of(i * ev_chunk, ev_chunk), ev_chunk)
        return pltpu.make_async_copy(ev_hbm.at[span], ev.at[span], ev_sem.at[i])

    def queue_copy(i):
        span = pl.ds(pl.multiple_of(i * slot_block, slot_block), slot_block)
        return pltpu.make_async_copy(queue_hbm.at[span], queue.at[span], queue_sem.at[i])

    partner = me + 1 - 2 * lax.rem(me, 2)

    def mem_peer(k):
        return (lax.rem(me + k, n), mf)

    def feat_peer(k):
        return (me, lax.rem(mf + k, nf))

    def block_id(i):
        return lax.rem(me + n - i, n) if i % 2 == 0 else lax.rem(partner + n - (i - 1), n)

    barrier = pltpu.get_barrier_semaphore()
    for k in range(1, n):
        pl.semaphore_signal(barrier, inc=1, device_id=mem_peer(k), device_id_type=MESH)
    for k in range(1, nf):
        pl.semaphore_signal(barrier, inc=1, device_id=feat_peer(k), device_id_type=MESH)
    for i in range(n_ev):
        ev_copy(i).start()
    for i in range(n_blk):
        queue_copy(i).start()

    def own_span(m):
        return pl.ds(pl.multiple_of(m * own, own), own)

    q_all[own_span(me), :] = probe_ref[...]
    t_all[me] = target_ref[...]
    pl.semaphore_wait(barrier, n - 1 + nf - 1)

    def remote(src, dst, ss, rs, to):
        return pltpu.make_async_remote_copy(
            src_ref=src, dst_ref=dst, send_sem=ss, recv_sem=rs, device_id=to, device_id_type=MESH
        )

    t_copies = [
        remote(target_ref, t_all.at[me], t_ss.at[k], t_rs.at[k], mem_peer(k)) for k in range(1, n)
    ]
    q_copies = {
        k: remote(probe_ref, q_all.at[own_span(me)], q_ss.at[k], q_rs.at[k], mem_peer(k))
        for k in range(2, n, 2)
    }
    q_copies[1] = remote(
        probe_ref, q_all.at[own_span(me)], q_ss.at[1], q_rs.at[1], (partner, mf)
    )
    for a in q_copies.values():
        a.start()
    for a in t_copies:
        a.start()

    events_of = ev_rows // sessions
    c1 = 0.7978845608028654
    c2 = c1 * 0.044715

    def encode(i, carry):
        ev_copy(i).wait()
        rows = ev[pl.ds(pl.multiple_of(i * ev_chunk, ev_chunk), ev_chunk), :]
        x = jnp.dot(rows, w_in_ref[...], preferred_element_type=jnp.float32)
        t = jnp.tanh(x * (c1 + c2 * (x * x)))
        y = x * t + x
        y = y.reshape(ev_chunk // events_of, events_of, y.shape[1])
        mean = jnp.sum(y, axis=1) * (0.5 / events_of)
        s = ev_chunk // events_of
        pooled[pl.ds(pl.multiple_of(i * s, s), s), :] = mean.astype(jnp.bfloat16)
        return carry

    lax.fori_loop(0, n_ev, encode, 0)
    partial[...] = jnp.dot(pooled[...], w_out_ref[...], preferred_element_type=jnp.float32)

    def part_span(f):
        return pl.ds(pl.multiple_of(f * part_rows, part_rows), part_rows)

    p_copies = []
    for k in range(1, nf):
        to = feat_peer(k)
        p_copies.append(
            remote(partial.at[part_span(to[1])], part_in.at[k], p_ss.at[k], p_rs.at[k], to)
        )
        p_copies[-1].start()

    for k in range(2, n, 2):
        q_copies[k].wait_recv()
        span = own_span(block_id(k))
        q_copies[k + 1] = remote(
            q_all.at[span], q_all.at[span], q_ss.at[k + 1], q_rs.at[k + 1], (partner, mf)
        )
        q_copies[k + 1].start()
    for a in t_copies:
        a.wait()

    diag = lax.broadcasted_iota(jnp.int32, (own, own), 0) == lax.broadcasted_iota(
        jnp.int32, (own, own), 1
    )

    def as_column(row):
        wide = jnp.broadcast_to(row, (own, own))
        return jnp.sum(jnp.where(diag, wide, 0.0), axis=1, keepdims=True)

    for j in range(n):
        local = as_column(t_all[j].astype(jnp.float32)).astype(jnp.int32) - me * slots
        pos[j * own : (j + 1) * own, :] = jnp.broadcast_to(local, (own, 128))

    acc[...] = jnp.zeros(acc.shape, jnp.float32)

    def pick(b, carry):
        queue_copy(b).wait()
        kb = queue[pl.ds(pl.multiple_of(b * slot_block, slot_block), slot_block), :]
        for c in range(rows_q // q_chunk):
            rs = slice(c * q_chunk, (c + 1) * q_chunk)
            at = lax.broadcasted_iota(jnp.int32, (q_chunk, slot_block), 1)
            hit = at == (pos[rs, :1] - b * slot_block)
            acc[rs, :] += jnp.dot(
                jnp.where(hit, 1.0, 0.0).astype(jnp.bfloat16), kb, preferred_element_type=jnp.float32
            )
        return carry

    lax.fori_loop(0, n_blk, pick, 0)
    pair_out[...] = acc[...].astype(jnp.bfloat16)
    h_copies = []
    for k in range(1, n):
        to = mem_peer(k)
        h_copies.append(
            remote(pair_out.at[own_span(to[0])], pair_in.at[k], h_ss.at[k], h_rs.at[k], to)
        )
        h_copies[-1].start()

    for k in range(1, n, 2):
        q_copies[k].wait_recv()

    m_s[...] = jnp.full(m_s.shape, -jnp.inf, jnp.float32)
    l_s[...] = jnp.zeros(l_s.shape, jnp.float32)
    acc[...] = jnp.zeros(acc.shape, jnp.float32)
    scale2 = inverse_softness * log2e

    def attend(b, carry):
        kb = queue[pl.ds(pl.multiple_of(b * slot_block, slot_block), slot_block), :]
        for c in range(rows_q // q_chunk):
            rs = slice(c * q_chunk, (c + 1) * q_chunk)
            s = lax.dot_general(
                q_all[rs, :], kb, (((1,), (1,)), ((), ())), preferred_element_type=jnp.float32
            )
            m_old = m_s[rs, :1]
            m_new = jnp.maximum(m_old, jnp.max(s, axis=1, keepdims=True))
            p = jnp.exp2((s - m_new) * scale2)
            alpha = jnp.exp2((m_old - m_new) * scale2)
            m_s[rs, :] = jnp.broadcast_to(m_new, (q_chunk, 128))
            l_new = l_s[rs, :1] * alpha + jnp.sum(p, axis=1, keepdims=True)
            l_s[rs, :] = jnp.broadcast_to(l_new, (q_chunk, 128))
            acc[rs, :] = acc[rs, :] * alpha + jnp.dot(
                p.astype(jnp.bfloat16), kb, preferred_element_type=jnp.float32
            )
        return carry

    stage_a, stage_b = n_blk // 8, (5 * n_blk) // 8
    lax.fori_loop(0, stage_a, attend, 0)

    for a in p_copies:
        a.wait()
    raw = partial[part_span(mf), :]
    for k in range(1, nf):
        raw = raw + part_in[k]
    scaled = raw * lax.rsqrt(jnp.mean(raw * raw, axis=1, keepdims=True) + epsilon) / 16.0

    def key_span(m, f):
        return pl.ds(pl.multiple_of((m * nf + f) * part_rows, part_rows), part_rows)

    mine = key_span(me, mf)
    keys_ref[mine, :] = scaled.astype(jnp.bfloat16)
    far_feat = lax.rem(mf + nf // 2, nf)
    far = (me, far_feat)
    near = (me, mf + 1 - 2 * lax.rem(mf, 2))

    def to_same(span, ss, rs, i, to):
        a = remote(keys_ref.at[span], keys_ref.at[span], ss.at[i], rs.at[i], to)
        a.start()
        return a

    k_copies = {k: to_same(mine, k_ss, k_rs, k, mem_peer(k)) for k in range(2, n, 2)}
    k_copies[1] = to_same(mine, k_ss, k_rs, 1, (partner, mf))
    y_copies = {0: to_same(mine, y_ss, y_rs, 0, far)}
    c_copies = {0: to_same(mine, c_ss, c_rs, 0, near)}

    lax.fori_loop(stage_a, stage_b, attend, 0)

    for k in range(2, n, 2):
        k_copies[k].wait_recv()
        span = key_span(block_id(k), mf)
        k_copies[k + 1] = to_same(span, k_ss, k_rs, k + 1, (partner, mf))
        y_copies[k] = to_same(span, y_ss, y_rs, k, far)
        c_copies[k] = to_same(span, c_ss, c_rs, k, near)

    lax.fori_loop(stage_b, n_blk, attend, 0)

    gout[...] = acc[...].astype(jnp.bfloat16)
    g_copies = []
    for k in range(1, n):
        to = mem_peer(k)
        g_copies.append(remote(gout.at[own_span(to[0])], g_in.at[k], g_ss.at[k], g_rs.at[k], to))
        g_copies[-1].start()
    lane = lax.broadcasted_iota(jnp.int32, m_s.shape, 1)
    packed = jnp.where(lane == 0, m_s[...], l_s[...]).T
    for j in range(n):
        stat_out[j, 0:2, :] = packed[0:2, j * own : (j + 1) * own]
    s_copies = []
    for k in range(1, n):
        to = mem_peer(k)
        s_copies.append(remote(stat_out.at[to[0]], stat_in.at[k], s_ss.at[k], s_rs.at[k], to))
        s_copies[-1].start()

    for i in range(1, n, 2):
        k_copies[i].wait_recv()
        span = key_span(block_id(i), mf)
        y_copies[i] = to_same(span, y_ss, y_rs, i, far)
        c_copies[i] = to_same(span, c_ss, c_rs, i, near)

    paired = pair_out[own_span(me), :].astype(jnp.float32)
    for a in h_copies:
        a.wait()
    for k in range(1, n):
        paired = paired + pair_in[k].astype(jnp.float32)
    score = jnp.sum(probe_ref[...].astype(jnp.float32) * paired, axis=1, keepdims=True)
    score = jnp.sum(
        jnp.where(diag, jnp.broadcast_to(score, (own, own)), 0.0), axis=0, keepdims=True
    )

    order = [0] + list(range(2, n, 2)) + list(range(1, n, 2))
    for i in order:
        y_copies[i].wait_recv()
        c_copies[n + i] = to_same(key_span(block_id(i), far_feat), c_ss, c_rs, n + i, near)

    for a in s_copies:
        a.wait()
    stats = [stat_out[me]] + [stat_in[k] for k in range(1, n)]
    top = stats[0][0:1, :]
    for st in stats[1:]:
        top = jnp.maximum(top, st[0:1, :])
    powers = [jnp.exp2((st[0:1, :] - top) * scale2) for st in stats]
    total = stats[0][1:2, :] * powers[0]
    for st, w in zip(stats[1:], powers[1:]):
        total = total + st[1:2, :] * w
    loss_ref[...] = (top - score) * inverse_softness + jnp.log(total)
    grad = acc[own_span(me), :] * as_column(powers[0] / total)
    for k in range(1, n):
        g_copies[k - 1].wait()
        grad = grad + g_in[k].astype(jnp.float32) * as_column(powers[k] / total)
    grad_ref[...] = inverse_softness * (grad - paired)

    for a in list(q_copies.values()) + list(k_copies.values()) + list(y_copies.values()):
        a.wait_send()
    for a in c_copies.values():
        a.wait()


def fill_kernel(
    block, start_ref, keys_hbm, queue_ref, loss_in, grad_in,
    loss_ref, grad_ref, out_hbm,
    keys, rolled, merged, keys_sem, out_sem,
):
    start = start_ref[0]
    count = keys.shape[0]
    slots, width = queue_ref.shape
    phase = jnp.bitwise_and(start, 15)
    blocks = slots // block
    here = (start < slots) & (start + count > 0)
    keys_copy = pltpu.make_async_copy(keys_hbm, keys, keys_sem)

    @pl.when(here)
    def _():
        keys_copy.start()

    def spans(i):
        return slice(i * block, (i + 1) * block)

    def inside(i):
        return (i * block < start + count) & ((i + 1) * block > start)

    def plain(i):
        return pltpu.make_async_copy(queue_ref.at[spans(i)], out_hbm.at[spans(i)], out_sem.at[i])

    for i in range(blocks):

        @pl.when(jnp.logical_not(inside(i)))
        def _():
            plain(i).start()

    loss_ref[...] = loss_in[...]
    grad_ref[...] = grad_in[...]

    @pl.when(here)
    def _():
        keys_copy.wait()
        tile = min(256, count)
        for c in range(count // tile + 1):
            lo = max(c * tile - 16, 0)
            hi = min(c * tile + tile, count)
            x = keys[lo:hi, :].astype(jnp.float32)
            if c == 0:
                x = jnp.concatenate([jnp.zeros((16, width), jnp.float32), x], axis=0)
            if c == count // tile:
                x = jnp.concatenate([x, jnp.zeros((16, width), jnp.float32)], axis=0)
            x = pltpu.roll(x, phase, 0)[16:, :]
            at = block + c * tile
            rolled[at : at + x.shape[0], :] = x.astype(jnp.bfloat16)

    for i in range(blocks):

        @pl.when(inside(i))
        def _():
            at = pl.multiple_of(block + i * block - (start - phase), 16)
            row = lax.broadcasted_iota(jnp.int32, (block, width), 0) + (i * block - start)
            take = (row >= 0) & (row < count)
            new = rolled[pl.ds(at, block), :].astype(jnp.float32)
            old = queue_ref[spans(i), :].astype(jnp.float32)
            merged[spans(i), :] = jnp.where(take, new, old).astype(jnp.bfloat16)
            pltpu.make_async_copy(
                merged.at[spans(i)], out_hbm.at[spans(i)], out_sem.at[i]
            ).start()

    for i in range(blocks):
        plain(i).wait()


def shards(events, w_in, w_out, probe_vectors, key_queue, target_position, pointer):
    n, nf = lax.axis_size("mem"), lax.axis_size("feat")
    sessions, per, depth = events.shape
    own, width = probe_vectors.shape
    slots = key_queue.shape[0]
    rows_q = own * n
    hidden = w_in.shape[1]
    flat = events.reshape(sessions * per, depth)
    ev_chunk = min(1024, flat.shape[0])
    slot_block = min(1024, slots)
    q_chunk = min(256, rows_q)
    part_rows = sessions // nf
    f32, bf16 = jnp.float32, jnp.bfloat16
    dma = pltpu.SemaphoreType.DMA
    loss, grad, keys = pl.pallas_call(
        functools.partial(step_kernel, n, nf, ev_chunk, slot_block, q_chunk),
        out_shape=(
            jax.ShapeDtypeStruct((1, own), f32),
            jax.ShapeDtypeStruct((own, width), f32),
            jax.ShapeDtypeStruct((sessions * n, width), bf16),
        ),
        in_specs=[ANY, VMEM, VMEM, VMEM, ANY, VMEM],
        out_specs=(VMEM, VMEM, VMEM),
        scratch_shapes=[
            pltpu.VMEM(flat.shape, bf16),
            pltpu.VMEM(key_queue.shape, bf16),
            pltpu.VMEM((rows_q, width), bf16),
            pltpu.VMEM((n, 1, own), jnp.int32),
            pltpu.VMEM((sessions, hidden), bf16),
            pltpu.VMEM((sessions, width), f32),
            pltpu.VMEM((nf, part_rows, width), f32),
            pltpu.VMEM((rows_q, 128), jnp.int32),
            pltpu.VMEM((rows_q, 128), f32),
            pltpu.VMEM((rows_q, 128), f32),
            pltpu.VMEM((rows_q, width), f32),
            pltpu.VMEM((rows_q, width), bf16),
            pltpu.VMEM((n, own, width), bf16),
            pltpu.VMEM((n, 4, own), f32),
            pltpu.VMEM((n, 4, own), f32),
            pltpu.VMEM((rows_q, width), bf16),
            pltpu.VMEM((n, own, width), bf16),
            dma((flat.shape[0] // ev_chunk,)),
            dma((slots // slot_block,)),
            dma((n,)), dma((n,)), dma((n,)), dma((n,)),
            dma((nf,)), dma((nf,)),
            dma((n,)), dma((n,)),
            dma((n,)), dma((n,)),
            dma((2 * n,)), dma((2 * n,)),
            dma((n,)), dma((n,)),
            dma((n,)), dma((n,)),
            dma((n,)), dma((n,)),
        ],
        compiler_params=pltpu.CompilerParams(
            collective_id=0, has_side_effects=True, vmem_limit_bytes=56 * 1024 * 1024
        ),
        name="step",
    )(flat, w_in, w_out, probe_vectors, key_queue, target_position.reshape(1, own))

    slots_total = slots * n
    start = lax.rem(pointer - lax.axis_index("mem") * slots + slots_total, slots_total)
    count = sessions * n
    start = jnp.where(start > slots_total - count, start - slots_total, start)
    block = min(512, slots)
    loss, grad, new_memory = pl.pallas_call(
        functools.partial(fill_kernel, block),
        out_shape=(
            jax.ShapeDtypeStruct((1, own), f32),
            jax.ShapeDtypeStruct((own, width), f32),
            jax.ShapeDtypeStruct(key_queue.shape, bf16),
        ),
        in_specs=[pl.BlockSpec(memory_space=pltpu.SMEM), HBM, VMEM, VMEM, VMEM],
        out_specs=(VMEM, VMEM, HBM),
        scratch_shapes=[
            pltpu.VMEM((count, width), bf16),
            pltpu.VMEM((count + 2 * block + 16, width), bf16),
            pltpu.VMEM(key_queue.shape, bf16),
            dma,
            dma((slots // block,)),
        ],
        compiler_params=pltpu.CompilerParams(vmem_limit_bytes=32 * 1024 * 1024),
        name="fill",
    )(start, keys, key_queue, loss, grad)
    return (loss.reshape(own), grad, new_memory)


def solution(mesh):
    placed = (
        P("mem", None, None),
        P(None, "feat"),
        P("feat", None),
        P(("mem", "feat"), None),
        P("mem", None),
        P(("mem", "feat")),
        P(),
    )
    return jax.shard_map(
        shards,
        mesh=mesh,
        in_specs=placed,
        out_specs=(P(("mem", "feat")), P(("mem", "feat"), None), P("mem", None)),
        check_vma=False,
    )
```
